512 devices in a mesh: dp: 8 (over y, z_hi), tensor: 64 (over x, z_lo, core).
Axes of the slice: x: 4, y: 4, z: 16 (z_hi: 2, z_lo: 8; z = z_hi * 8 + z_lo), core: 2. Of those that a mesh axis runs over, the one named last changes fastest.
Arguments:
- tokens: bfloat16 [8192, 8192], P('dp', 'tensor'), may hold values from -6 to 6
- first_up: bfloat16 [64, 128, 128], P('tensor'), may hold values from -0.5 to 0.5
- second_up: bfloat16 [128, 64, 256], P('tensor'), may hold values from -0.75 to 0.75
- first_down: bfloat16 [128, 256, 64], P('tensor'), may hold values from -0.375 to 0.375
- second_down: bfloat16 [64, 128, 128], P('tensor'), may hold values from -0.5 to 0.5
- out_grad: bfloat16 [8192, 8192], P('dp', 'tensor'), may hold values from -6 to 6
Outputs:
- output: bfloat16 [8192, 8192], P('dp', 'tensor')
- tokens_grad: bfloat16 [8192, 8192], P('dp', 'tensor')
- first_up_grad: float32 [64, 128, 128], P('tensor')
- second_up_grad: float32 [128, 64, 256], P('tensor')
- first_down_grad: float32 [128, 256, 64], P('tensor')
- second_down_grad: float32 [64, 128, 128], P('tensor')
The draws below stay inside these ranges and needn't reach their ends.
All inputs are finite; a program needn't handle non-finite values.
Results may differ from the reference program's by a relative error of at most 0.0095.
Values may be sent and summed in bfloat16 or wider, within the bound.
A program may use at most 64 MiB of HBM per device.

```python
import math
import jax
import jax.numpy as jnp
from jax import lax

D = 8192
BLK = 128
TOK = 1024
NB = 64
HB = 256
TOKENS = 8192
N_DP = 8


def shard_levels(stream_key, shape, shards, low, high):
    def one(axis_at, parts):
        draws = jax.random.uniform(jax.random.fold_in(jax.random.fold_in(stream_key, 6), axis_at), (parts,), jnp.float32, low / len(shards), high / len(shards))
        return jnp.repeat(jnp.exp(draws), shape[axis_at] // parts).reshape((-1,) + (1,) * (len(shape) - axis_at - 1))

    gain = one(*shards[0])
    for cut in shards[1:]:
        gain = gain * one(*cut)
    return gain


def scatter_about(stream_key, dims, scale, most, cuts=(), kind=jnp.bfloat16):
    result = scale * jax.random.normal(stream_key, dims, jnp.float32)
    if cuts:
        result = result * shard_levels(stream_key, dims, cuts, -0.22, 0.18)
    return jnp.clip(result, -most, most).astype(kind)


def setup_inputs(seed: int = 0) -> dict:
    arg_keys = jax.random.split(jax.random.key(seed), 7)
    tokens = scatter_about(arg_keys[0], (TOKENS, D), 1.0, 6.0, ((0, 8), (1, 64)))
    first_up = scatter_about(arg_keys[1], (NB, BLK, BLK), BLK ** -0.5, 0.5, ((0, 64),))
    second_up = scatter_about(arg_keys[2], (BLK, NB, HB), NB ** -0.5, 0.75, ((0, 64),))
    first_down = scatter_about(arg_keys[3], (BLK, HB, NB), HB ** -0.5, 0.375, ((0, 64),))
    second_down = scatter_about(arg_keys[4], (NB, BLK, BLK), BLK ** -0.5, 0.5, ((0, 64),))
    out_grad = scatter_about(arg_keys[5], (TOKENS, D), 1.0, 6.0, ((0, 8), (1, 64)))
    return {"tokens": tokens, "first_up": first_up, "second_up": second_up, "first_down": first_down, "second_down": second_down, "out_grad": out_grad}


def cdf_part(value):
    return 0.5 * (1.0 + jax.scipy.special.erf(value / math.sqrt(2.0)))

def gelu_deriv(value):
    return cdf_part(value) + value * jnp.exp(-0.5 * value * value) / math.sqrt(2.0 * math.pi)

def reference(tokens, first_up, second_up, first_down, second_down, out_grad):
    f32 = jnp.float32
    bf16 = jnp.bfloat16
    wu1 = first_up.astype(f32)
    wu2 = second_up.astype(f32)
    wd1 = first_down.astype(f32)
    wd2 = second_down.astype(f32)
    groups_x = tokens.reshape(N_DP, TOK, NB, BLK)
    groups_e = out_grad.reshape(N_DP, TOK, NB, BLK)

    def group_step(carry, pair):
        xblk, eblk = pair
        xfl = xblk.astype(f32)
        efl = eblk.astype(f32)
        upper = jnp.einsum('tbi,bij->tbj', xfl, wu1).astype(bf16)
        pre = jnp.einsum('tbj,jbo->tjo', upper.astype(f32), wu2).astype(bf16)
        prefl = pre.astype(f32)
        act = (prefl * cdf_part(prefl)).astype(bf16)
        zeta = jnp.einsum('tjo,job->tbj', act.astype(f32), wd1).astype(bf16)
        outv = jnp.einsum('tbj,bjk->tbk', zeta.astype(f32), wd2).astype(bf16)
        grad_d2 = jnp.einsum('tbj,tbk->bjk', zeta.astype(f32), efl)
        dzeta = jnp.einsum('tbk,bjk->tbj', efl, wd2).astype(bf16)
        grad_d1 = jnp.einsum('tjo,tbj->job', act.astype(f32), dzeta.astype(f32))
        dact = jnp.einsum('tbj,job->tjo', dzeta.astype(f32), wd1)
        dpre = (dact * gelu_deriv(prefl)).astype(bf16)
        grad_u2 = jnp.einsum('tbj,tjo->jbo', upper.astype(f32), dpre.astype(f32))
        dupper = jnp.einsum('tjo,jbo->tbj', dpre.astype(f32), wu2).astype(bf16)
        grad_u1 = jnp.einsum('tbi,tbj->bij', xfl, dupper.astype(f32))
        dxval = jnp.einsum('tbj,bij->tbi', dupper.astype(f32), wu1).astype(bf16)
        carry = (carry[0] + grad_u1, carry[1] + grad_u2, carry[2] + grad_d1, carry[3] + grad_d2)
        return (carry, (outv, dxval))
    start = (jnp.zeros((NB, BLK, BLK), f32), jnp.zeros((BLK, NB, HB), f32), jnp.zeros((BLK, HB, NB), f32), jnp.zeros((NB, BLK, BLK), f32))
    grads, stacked = lax.scan(group_step, start, (groups_x, groups_e))
    output = stacked[0].reshape(TOKENS, D)
    tokens_grad = stacked[1].reshape(TOKENS, D)
    return (output, tokens_grad, grads[0], grads[1], grads[2], grads[3])
```

```python
import math

import jax
import jax.numpy as jnp
from jax import lax
from jax.sharding import PartitionSpec as P

F32 = jnp.float32
BF16 = jnp.bfloat16


def mm(spec, a, b, dtype=BF16):
    return jnp.einsum(spec, a, b, preferred_element_type=F32).astype(dtype)


def cdf_part(value):
    return 0.5 * (1.0 + jax.scipy.special.erf(value / math.sqrt(2.0)))


def gelu_deriv(value):
    return cdf_part(value) + value * jnp.exp(-0.5 * value * value) / math.sqrt(2.0 * math.pi)


def row_picks(peers, cols):
    rows = peers * 2 * cols
    row = lax.broadcasted_iota(jnp.int32, (peers * cols, rows), 1)
    unit = lax.broadcasted_iota(jnp.int32, (peers * cols, rows), 0)
    flat = []
    for which in range(2):
        flat.append((row == (unit // cols) * (2 * cols) + which * cols + unit % cols).astype(BF16))
    row = lax.broadcasted_iota(jnp.int32, (cols, peers, rows), 2)
    peer = lax.broadcasted_iota(jnp.int32, (cols, peers, rows), 1)
    col = lax.broadcasted_iota(jnp.int32, (cols, peers, rows), 0)
    grouped = [(row == peer * (2 * cols) + which * cols + col).astype(BF16) for which in range(2)]
    return flat, grouped


def exchange(rows, peers):
    n, t = rows.shape
    out = lax.all_to_all(rows.reshape(peers, n // peers, t), "tensor", split_axis=0, concat_axis=0, tiled=True)
    return out.reshape(n, t)


def group_sum(parts):
    groups = lax.axis_size("dp")
    flat = jnp.concatenate([p.astype(BF16).reshape(groups, -1, 128) for p in parts], axis=1)
    landed = lax.all_to_all(flat, "dp", split_axis=0, concat_axis=0, tiled=True)
    total = jnp.sum(landed.astype(F32), axis=0, keepdims=True).astype(BF16)
    spread = lax.all_to_all(
        jnp.broadcast_to(total, flat.shape), "dp", split_axis=0, concat_axis=0, tiled=True
    )
    out, at = [], 0
    for p in parts:
        n = p.size // groups // 128
        out.append(spread[:, at : at + n].astype(F32).reshape(p.shape))
        at += n
    return out


def shards(tokens, first_up, second_up, first_down, second_down, out_grad):
    peers = lax.axis_size("tensor")
    t = tokens.shape[0]
    cols, _, hidden = second_up.shape
    fu, sd = first_up[0], second_down[0]
    (p0, p1), (q0, q1) = row_picks(peers, cols)

    both = jnp.concatenate([tokens, out_grad], axis=1)
    w_in = jnp.concatenate([mm("jr,ij->ri", p0, fu), mm("jr,jk->rk", p1, sd)], axis=1)
    sent = mm("rc,tc->rt", w_in, both)
    x = exchange(sent, peers)

    w_pre = mm("jbr,jbo->jor", q0, second_up).reshape(cols * hidden, -1)
    w_dact = mm("jbr,job->jor", q1, first_down).reshape(cols * hidden, -1)
    w_z = mm("jbr,job->rjo", q0, first_down).reshape(-1, cols * hidden)
    w_du = mm("jbr,jbo->rjo", q1, second_up).reshape(-1, cols * hidden)
    w_out = jnp.concatenate([mm("jr,jk->rk", p0, sd), mm("jr,ij->ri", p1, fu)], axis=1)

    pre = mm("or,rt->ot", w_pre, x).astype(F32)
    act = (pre * cdf_part(pre)).astype(BF16)
    dact = mm("or,rt->ot", w_dact, x, F32)
    dpre = (dact * gelu_deriv(pre)).astype(BF16)
    back = mm(
        "rc,ct->rt", jnp.concatenate([w_z, w_du], axis=1), jnp.concatenate([act, dpre], axis=0)
    )
    r = exchange(back, peers)

    u_cols = mm("jbr,rt->jbt", q0, x)
    dz_cols = mm("jbr,rt->jbt", q1, x)
    act3 = act.reshape(cols, hidden, t)
    dpre3 = dpre.reshape(cols, hidden, t)
    grad_d1 = mm("jot,jbt->job", act3, dz_cols, F32)
    grad_u2 = mm("jbt,jot->jbo", u_cols, dpre3, F32)

    z_rows = mm("jr,rt->jt", p0, r)
    du_rows = mm("jr,rt->jt", p1, r)
    grad_d2 = mm("jt,tk->jk", z_rows, out_grad, F32)[None]
    grad_u1 = mm("ti,jt->ij", tokens, du_rows, F32)[None]
    outs = mm("rt,rc->tc", r, w_out)
    width = tokens.shape[1]
    g_u1, g_u2, g_d1, g_d2 = group_sum([grad_u1, grad_u2, grad_d1, grad_d2])
    return (outs[:, :width], outs[:, width:], g_u1, g_u2, g_d1, g_d2)


def solution(mesh):
    cols = P("dp", "tensor")
    blocks = P("tensor", None, None)
    return jax.shard_map(
        shards,
        mesh=mesh,
        in_specs=(cols, blocks, blocks, blocks, blocks, cols),
        out_specs=(cols, cols, blocks, blocks, blocks, blocks),
        check_vma=False,
    )
```

```python
import functools
import math

import jax
import jax.numpy as jnp
from jax import lax
from jax.experimental import pallas as pl
from jax.experimental.pallas import tpu as pltpu
from jax.sharding import PartitionSpec as P

F32 = jnp.float32
BF16 = jnp.bfloat16


def mm(spec, a, b, dtype=BF16):
    return jnp.einsum(spec, a, b, preferred_element_type=F32).astype(dtype)


def cdf_part(value):
    return 0.5 * (1.0 + jax.scipy.special.erf(value / math.sqrt(2.0)))


def gelu_deriv(value):
    return cdf_part(value) + value * jnp.exp(-0.5 * value * value) / math.sqrt(2.0 * math.pi)


def row_picks(peers, cols):
    rows = peers * 2 * cols
    row = lax.broadcasted_iota(jnp.int32, (peers * cols, rows), 1)
    unit = lax.broadcasted_iota(jnp.int32, (peers * cols, rows), 0)
    flat = []
    for which in range(2):
        flat.append((row == (unit // cols) * (2 * cols) + which * cols + unit % cols).astype(BF16))
    row = lax.broadcasted_iota(jnp.int32, (cols, peers, rows), 2)
    peer = lax.broadcasted_iota(jnp.int32, (cols, peers, rows), 1)
    col = lax.broadcasted_iota(jnp.int32, (cols, peers, rows), 0)
    grouped = [(row == peer * (2 * cols) + which * cols + col).astype(BF16) for which in range(2)]
    return flat, grouped


def greet(axis_sizes):
    barrier = pltpu.get_barrier_semaphore()
    for axis, n in axis_sizes:
        me = lax.axis_index(axis)

        def tell(k, carry, axis=axis, n=n, me=me):
            pl.semaphore_signal(
                barrier, inc=1, device_id={axis: (me + k) % n}, device_id_type=pl.DeviceIdType.MESH
            )
            return carry

        lax.fori_loop(1, n, tell, 0)


def greeted(axis_sizes):
    pl.semaphore_wait(pltpu.get_barrier_semaphore(), sum(n - 1 for _, n in axis_sizes))


def remote(src, dst, send, recv, axis, peer):
    return pltpu.make_async_remote_copy(
        src_ref=src,
        dst_ref=dst,
        send_sem=send,
        recv_sem=recv,
        device_id={axis: peer},
        device_id_type=pl.DeviceIdType.MESH,
    )


def start_exchange(src, dst, sems, n):
    me = lax.axis_index("tensor")

    def push(i, carry):
        step = (i % 8 // 2) * (n // 4) + ((i // 8 + n // 16) % (n // 8)) * 2 + i % 2
        peer = (me + step) % n
        remote(src.at[peer], dst.at[me], sems.at[0], sems.at[1], "tensor", peer).start()
        return carry

    lax.fori_loop(0, n // 2, push, 0)
    lax.fori_loop(n // 2 + 1, n, push, 0)
    own = pltpu.make_async_copy(src.at[me], dst.at[me], sems.at[2])
    own.start()
    return own


def end_exchange(src, dst, sems, n, own):
    own.wait()
    span = pl.ds(0, n - 1)
    all_of = remote(src.at[span], dst.at[span], sems.at[0], sems.at[1], "tensor", 0)
    all_of.wait_recv()
    all_of.wait_send()


def sum_scatter(flat, land, sems, n):
    me = lax.axis_index("dp")

    def push(k, carry):
        peer = (me + k) % n
        remote(flat.at[peer], land.at[me], sems.at[0], sems.at[1], "dp", peer).start()
        return carry

    lax.fori_loop(1, n, push, 0)
    land[pl.ds(me, 1)] = flat[pl.ds(me, 1)]


def sum_spread(flat, land, total, gath, sems, n):
    me = lax.axis_index("dp")
    span = pl.ds(0, n - 1)
    first = remote(flat.at[span], land.at[span], sems.at[0], sems.at[1], "dp", 0)
    first.wait_recv()
    acc = land[0].astype(F32)
    for k in range(1, n):
        acc = acc + land[k].astype(F32)
    total[...] = acc.astype(BF16)
    gath[pl.ds(me, 1)] = acc.astype(BF16)[None]

    def push(k, carry):
        peer = (me + k) % n
        remote(total, gath.at[me], sems.at[2], sems.at[3], "dp", peer).start()
        return carry

    lax.fori_loop(1, n, push, 0)
    first.wait_send()


def sum_end(gath, sems, n):
    span = pl.ds(0, n - 1)
    last = remote(gath.at[span], gath.at[span], sems.at[2], sems.at[3], "dp", 0)
    last.wait_recv()
    last.wait_send()


def dot_nt(a, b):
    return lax.dot_general(a, b, (((1,), (1,)), ((), ())), preferred_element_type=F32)


def dot(a, b):
    return jnp.dot(a, b, preferred_element_type=F32)


def first_kernel(n, src, dst, sems):
    greet((("tensor", n),))
    greeted((("tensor", n),))
    own = start_exchange(src, dst, sems, n)
    end_exchange(src, dst, sems, n, own)


def middle_kernel(n, g, src, x, act, dpre, q0, q1, dst, out, flat, land, total, gath, sems, dsems):
    axes = (("tensor", n), ("dp", g))
    cols = q0.shape[0]
    rows, width = flat.shape[2:]
    greet(axes)
    for j in range(cols):
        u = dot(q0[j], x[...]).astype(BF16)
        dz = dot(q1[j], x[...]).astype(BF16)
        flat[:, j] = dot_nt(u, dpre[j]).reshape(g, rows, width).astype(BF16)
        flat[:, cols + j] = dot_nt(dz, act[j]).reshape(g, rows, width).astype(BF16)
    greeted(axes)
    sum_scatter(flat, land, dsems, g)
    own = start_exchange(src, dst, sems, n)
    sum_spread(flat, land, total, gath, dsems, g)
    sum_end(gath, dsems, g)
    for m in range(2 * cols):
        out[m] = gath[:, m].astype(F32).reshape(g * rows, width)
    end_exchange(src, dst, sems, n, own)


def last_kernel(g, r, tok, og, p0, p1, out, flat, land, total, gath, dsems):
    axes = (("dp", g),)
    rows, width = flat.shape[2:]
    greet(axes)
    z = dot(p0[...], r[...]).astype(BF16)
    flat[:, 0] = dot(z, og[...]).reshape(g, rows, width).astype(BF16)
    du = dot(p1[...], r[...]).astype(BF16)
    flat[:, 1] = dot(du, tok[...]).T.reshape(g, rows, width).astype(BF16)
    greeted(axes)
    sum_scatter(flat, land, dsems, g)
    sum_spread(flat, land, total, gath, dsems, g)
    sum_end(gath, dsems, g)
    for m in range(2):
        out[m] = gath[:, m].astype(F32).reshape(g * rows, width)


def sum_scratch(g, mats, rows, width):
    return [
        pltpu.VMEM((g, mats, rows, width), BF16),
        pltpu.VMEM((g, mats, rows, width), BF16),
        pltpu.VMEM((mats, rows, width), BF16),
        pltpu.VMEM((g, mats, rows, width), BF16),
    ]


def kernel_call(body, ins, outs, scratch, ident):
    vmem = pl.BlockSpec(memory_space=pltpu.VMEM)
    return pl.pallas_call(
        body,
        out_shape=outs,
        in_specs=[vmem] * len(ins),
        out_specs=[vmem] * len(outs),
        scratch_shapes=scratch,
        compiler_params=pltpu.CompilerParams(collective_id=ident, has_side_effects=True),
    )(*ins)


def shards(tokens, first_up, second_up, first_down, second_down, out_grad):
    peers = lax.axis_size("tensor")
    t = tokens.shape[0]
    cols, _, hidden = second_up.shape
    fu, sd = first_up[0], second_down[0]
    (p0, p1), (q0, q1) = row_picks(peers, cols)

    both = jnp.concatenate([tokens, out_grad], axis=1)
    w_in = jnp.concatenate([mm("jr,ij->ri", p0, fu), mm("jr,jk->rk", p1, sd)], axis=1)
    sent = mm("rc,tc->rt", w_in, both)
    groups = lax.axis_size("dp")
    block = jax.ShapeDtypeStruct((peers, 2 * cols, t), BF16)
    links = pltpu.SemaphoreType.DMA((3,))
    sums = pltpu.SemaphoreType.DMA((4,))
    (x,) = kernel_call(
        functools.partial(first_kernel, peers), [sent.reshape(block.shape)], [block], [links], 0
    )
    x = x.reshape(sent.shape)

    w_pre = mm("jbr,jbo->jor", q0, second_up).reshape(cols * hidden, -1)
    w_dact = mm("jbr,job->jor", q1, first_down).reshape(cols * hidden, -1)
    w_z = mm("jbr,job->rjo", q0, first_down).reshape(-1, cols * hidden)
    w_du = mm("jbr,jbo->rjo", q1, second_up).reshape(-1, cols * hidden)
    w_out = jnp.concatenate([mm("jr,jk->rk", p0, sd), mm("jr,ij->ri", p1, fu)], axis=1)

    pre = mm("or,rt->ot", w_pre, x).astype(F32)
    act = (pre * cdf_part(pre)).astype(BF16)
    dact = mm("or,rt->ot", w_dact, x, F32)
    dpre = (dact * gelu_deriv(pre)).astype(BF16)
    back = mm(
        "rc,ct->rt", jnp.concatenate([w_z, w_du], axis=1), jnp.concatenate([act, dpre], axis=0)
    )
    r, mids = kernel_call(
        functools.partial(middle_kernel, peers, groups),
        [
            back.reshape(block.shape),
            x,
            act.reshape(cols, hidden, t),
            dpre.reshape(cols, hidden, t),
            q0,
            q1,
        ],
        [block, jax.ShapeDtypeStruct((2 * cols, peers, hidden), F32)],
        sum_scratch(groups, 2 * cols, peers // groups, hidden) + [links, sums],
        1,
    )
    r = r.reshape(sent.shape)
    width = tokens.shape[1]
    (ends,) = kernel_call(
        functools.partial(last_kernel, groups),
        [r, tokens, out_grad, p0, p1],
        [jax.ShapeDtypeStruct((2, width, width), F32)],
        sum_scratch(groups, 2, width // groups, width) + [sums],
        2,
    )
    outs = mm("rt,rc->tc", r, w_out)
    return (
        outs[:, :width],
        outs[:, width:],
        ends[1:],
        mids[:cols],
        mids[cols:].swapaxes(1, 2),
        ends[:1],
    )


def solution(mesh):
    cols = P("dp", "tensor")
    blocks = P("tensor", None, None)
    return jax.shard_map(
        shards,
        mesh=mesh,
        in_specs=(cols, blocks, blocks, blocks, blocks, cols),
        out_specs=(cols, cols, blocks, blocks, blocks, blocks),
        check_vma=False,
    )
```

```python
import functools
import math

import jax
import jax.numpy as jnp
from jax import lax
from jax.experimental import pallas as pl
from jax.experimental.pallas import tpu as pltpu
from jax.sharding import PartitionSpec as P

F32 = jnp.float32
BF16 = jnp.bfloat16


def mm(spec, a, b, dtype=BF16):
    return jnp.einsum(spec, a, b, preferred_element_type=F32).astype(dtype)


def cdf_part(value):
    return 0.5 * (1.0 + jax.scipy.special.erf(value / math.sqrt(2.0)))


def gelu_deriv(value):
    return cdf_part(value) + value * jnp.exp(-0.5 * value * value) / math.sqrt(2.0 * math.pi)


def row_picks(peers, cols):
    rows = peers * 2 * cols
    row = lax.broadcasted_iota(jnp.int32, (peers * cols, rows), 1)
    unit = lax.broadcasted_iota(jnp.int32, (peers * cols, rows), 0)
    flat = []
    for which in range(2):
        flat.append((row == (unit // cols) * (2 * cols) + which * cols + unit % cols).astype(BF16))
    row = lax.broadcasted_iota(jnp.int32, (cols, peers, rows), 2)
    peer = lax.broadcasted_iota(jnp.int32, (cols, peers, rows), 1)
    col = lax.broadcasted_iota(jnp.int32, (cols, peers, rows), 0)
    grouped = [(row == peer * (2 * cols) + which * cols + col).astype(BF16) for which in range(2)]
    return flat, grouped


def greet(axis_sizes):
    barrier = pltpu.get_barrier_semaphore()
    for axis, n in axis_sizes:
        me = lax.axis_index(axis)

        def tell(k, carry, axis=axis, n=n, me=me):
            pl.semaphore_signal(
                barrier, inc=1, device_id={axis: (me + k) % n}, device_id_type=pl.DeviceIdType.MESH
            )
            return carry

        lax.fori_loop(1, n, tell, 0)


def greeted(axis_sizes):
    pl.semaphore_wait(pltpu.get_barrier_semaphore(), sum(n - 1 for _, n in axis_sizes))


def remote(src, dst, send, recv, axis, peer):
    return pltpu.make_async_remote_copy(
        src_ref=src,
        dst_ref=dst,
        send_sem=send,
        recv_sem=recv,
        device_id={axis: peer},
        device_id_type=pl.DeviceIdType.MESH,
    )


def start_exchange(src, dst, sems, n, spans):
    me = lax.axis_index("tensor")

    def push(i, carry):
        step = (i % 8 // 2) * (n // 4) + ((i // 8 + n // 16) % (n // 8)) * 2 + i % 2
        peer = (me + step) % n
        remote(src.at[peer], dst.at[me], sems.at[0], sems.at[1], "tensor", peer).start()
        return carry

    for lo, hi in spans:
        lax.fori_loop(lo, hi, push, 0)


def keep_own(src, dst, sems):
    me = lax.axis_index("tensor")
    return pltpu.make_async_copy(src.at[me], dst.at[me], sems.at[2])


def end_exchange(src, dst, sems, n):
    keep_own(src, dst, sems).wait()
    span = pl.ds(0, n - 1)
    all_of = remote(src.at[span], dst.at[span], sems.at[0], sems.at[1], "tensor", 0)
    all_of.wait_recv()
    all_of.wait_send()


def sum_scatter(flat, land, sems, ny):
    me = lax.axis_index("dp")
    y, half = me // 2, me % 2

    def push(k, carry):
        peer = (y + k) % ny
        remote(flat.at[peer], land.at[y], sems.at[0], sems.at[1], "dp", peer * 2 + half).start()
        return carry

    lax.fori_loop(1, ny, push, 0)
    land[pl.ds(y, 1)] = flat[pl.ds(y, 1)]


def sum_swap(flat, land, pair, sems, ny):
    me = lax.axis_index("dp")
    span = pl.ds(0, ny - 1)
    first = remote(flat.at[span], land.at[span], sems.at[0], sems.at[1], "dp", 0)
    first.wait_recv()
    acc = land[0].astype(F32)
    for k in range(1, ny):
        acc = acc + land[k].astype(F32)
    pair[0] = acc.astype(BF16)
    other = me // 2 * 2 + (1 - me % 2)
    remote(pair.at[0], pair.at[1], sems.at[2], sems.at[3], "dp", other).start()
    first.wait_send()


def sum_spread(pair, total, gath, sems, ny):
    me = lax.axis_index("dp")
    y, half = me // 2, me % 2
    swap = remote(pair.at[0], pair.at[1], sems.at[2], sems.at[3], "dp", 0)
    swap.wait_recv()
    acc = (pair[0].astype(F32) + pair[1].astype(F32)).astype(BF16)
    total[...] = acc
    gath[pl.ds(y, 1)] = acc[None]

    def push(k, carry):
        peer = (y + k) % ny
        remote(total, gath.at[y], sems.at[4], sems.at[5], "dp", peer * 2 + half).start()
        return carry

    lax.fori_loop(1, ny, push, 0)
    swap.wait_send()


def sum_end(gath, out, sems, ny):
    span = pl.ds(0, ny - 1)
    last = remote(gath.at[span], gath.at[span], sems.at[4], sems.at[5], "dp", 0)
    last.wait_recv()
    for m in range(out.shape[0]):
        out[m] = gath[:, m].astype(F32).reshape(out.shape[1:])
    last.wait_send()


def dot_nt(a, b):
    return lax.dot_general(a, b, (((1,), (1,)), ((), ())), preferred_element_type=F32)


def dot(a, b):
    return jnp.dot(a, b, preferred_element_type=F32)


def dot_tn(a, b):
    return lax.dot_general(a, b, (((0,), (0,)), ((), ())), preferred_element_type=F32)


def first_kernel(n, src, dst, sems):
    greet((("tensor", n),))
    greeted((("tensor", n),))
    start_exchange(src, dst, sems, n, ((0, n // 2), (n // 2 + 1, n)))
    keep_own(src, dst, sems).start()
    end_exchange(src, dst, sems, n)


def rest_kernel(
    n, g, src, x, act, dpre, q0, q1, tok, og, p0, p1, w_out,
    output, tok_grad, mids, ends,
    dst, flat, land, pair, total, gath, flat2, land2, pair2, total2, gath2, links, sums, sums2,
):
    axes = (("tensor", n), ("dp", g))
    ny = g // 2
    cols = q0.shape[0]
    rows, hidden = flat.shape[2:]
    width = tok.shape[1]
    greet(axes)
    for j in range(cols):
        u = dot(q0[j], x[...]).astype(BF16)
        dz = dot(q1[j], x[...]).astype(BF16)
        flat[:, j] = dot_nt(u, dpre[j]).reshape(ny, rows, hidden).astype(BF16)
        flat[:, cols + j] = dot_nt(dz, act[j]).reshape(ny, rows, hidden).astype(BF16)
    greeted(axes)
    sum_scatter(flat, land, sums, ny)
    start_exchange(src, dst, links, n, ((0, n // 4), (n // 2 + 1, n)))
    keep_own(src, dst, links).start()
    sum_swap(flat, land, pair, sums, ny)
    start_exchange(src, dst, links, n, ((n // 4, n // 2),))
    sum_spread(pair, total, gath, sums, ny)
    sum_end(gath, mids, sums, ny)
    end_exchange(src, dst, links, n)

    r = dst[...].reshape(n * dst.shape[1], dst.shape[2])
    z = dot(p0[...], r).astype(BF16)
    flat2[:, 0] = dot(z, og[...]).reshape(ny, width // ny, width).astype(BF16)
    du = dot(p1[...], r).astype(BF16)
    flat2[:, 1] = dot(du, tok[...]).T.reshape(ny, width // ny, width).astype(BF16)
    sum_scatter(flat2, land2, sums2, ny)
    output[...] = dot_tn(r, w_out[:, :width]).astype(BF16)
    sum_swap(flat2, land2, pair2, sums2, ny)
    tok_grad[...] = dot_tn(r, w_out[:, width:]).astype(BF16)
    sum_spread(pair2, total2, gath2, sums2, ny)
    sum_end(gath2, ends, sums2, ny)


def sum_scratch(ny, mats, rows, width):
    return [
        pltpu.VMEM((ny, mats, rows, width), BF16),
        pltpu.VMEM((ny, mats, rows, width), BF16),
        pltpu.VMEM((2, mats, rows, width), BF16),
        pltpu.VMEM((mats, rows, width), BF16),
        pltpu.VMEM((ny, mats, rows, width), BF16),
    ]


def kernel_call(body, ins, outs, scratch, ident):
    vmem = pl.BlockSpec(memory_space=pltpu.VMEM)
    return pl.pallas_call(
        body,
        out_shape=outs,
        in_specs=[vmem] * len(ins),
        out_specs=[vmem] * len(outs),
        scratch_shapes=scratch,
        compiler_params=pltpu.CompilerParams(collective_id=ident, has_side_effects=True),
    )(*ins)


def shards(tokens, first_up, second_up, first_down, second_down, out_grad):
    peers = lax.axis_size("tensor")
    t = tokens.shape[0]
    cols, _, hidden = second_up.shape
    fu, sd = first_up[0], second_down[0]
    (p0, p1), (q0, q1) = row_picks(peers, cols)

    both = jnp.concatenate([tokens, out_grad], axis=1)
    w_in = jnp.concatenate([mm("jr,ij->ri", p0, fu), mm("jr,jk->rk", p1, sd)], axis=1)
    sent = mm("rc,tc->rt", w_in, both)
    groups = lax.axis_size("dp")
    block = jax.ShapeDtypeStruct((peers, 2 * cols, t), BF16)
    links = pltpu.SemaphoreType.DMA((3,))
    sums = pltpu.SemaphoreType.DMA((6,))
    (x,) = kernel_call(
        functools.partial(first_kernel, peers), [sent.reshape(block.shape)], [block], [links], 0
    )
    x = x.reshape(sent.shape)

    w_pre = mm("jbr,jbo->jor", q0, second_up).reshape(cols * hidden, -1)
    w_dact = mm("jbr,job->jor", q1, first_down).reshape(cols * hidden, -1)
    w_z = mm("jbr,job->rjo", q0, first_down).reshape(-1, cols * hidden)
    w_du = mm("jbr,jbo->rjo", q1, second_up).reshape(-1, cols * hidden)
    w_out = jnp.concatenate([mm("jr,jk->rk", p0, sd), mm("jr,ij->ri", p1, fu)], axis=1)

    pre = mm("or,rt->ot", w_pre, x).astype(F32)
    act = (pre * cdf_part(pre)).astype(BF16)
    dact = mm("or,rt->ot", w_dact, x, F32)
    dpre = (dact * gelu_deriv(pre)).astype(BF16)
    back = mm(
        "rc,ct->rt", jnp.concatenate([w_z, w_du], axis=1), jnp.concatenate([act, dpre], axis=0)
    )
    width = tokens.shape[1]
    ny = groups // 2
    output, tok_grad, mids, ends = kernel_call(
        functools.partial(rest_kernel, peers, groups),
        [
            back.reshape(block.shape),
            x,
            act.reshape(cols, hidden, t),
            dpre.reshape(cols, hidden, t),
            q0,
            q1,
            tokens,
            out_grad,
            p0,
            p1,
            w_out,
        ],
        [
            jax.ShapeDtypeStruct((t, width), BF16),
            jax.ShapeDtypeStruct((t, width), BF16),
            jax.ShapeDtypeStruct((2 * cols, peers, hidden), F32),
            jax.ShapeDtypeStruct((2, width, width), F32),
        ],
        [pltpu.VMEM(block.shape, BF16)]
        + sum_scratch(ny, 2 * cols, peers // ny, hidden)
        + sum_scratch(ny, 2, width // ny, width)
        + [links, sums, sums],
        1,
    )
    return (
        output,
        tok_grad,
        ends[1:],
        mids[:cols],
        mids[cols:].swapaxes(1, 2),
        ends[:1],
    )


def solution(mesh):
    cols = P("dp", "tensor")
    blocks = P("tensor", None, None)
    return jax.shard_map(
        shards,
        mesh=mesh,
        in_specs=(cols, blocks, blocks, blocks, blocks, cols),
        out_specs=(cols, cols, blocks, blocks, blocks, blocks),
        check_vma=False,
    )
```

```python
import functools
import math

import jax
import jax.numpy as jnp
import numpy as np
from jax import lax
from jax.experimental import pallas as pl
from jax.experimental.pallas import tpu as pltpu
from jax.sharding import PartitionSpec as P

F32 = jnp.float32
BF16 = jnp.bfloat16


def cdf_part(value):
    return 0.5 * (1.0 + jax.scipy.special.erf(value / math.sqrt(2.0)))


def row_orders(peers, cols):
    rows = peers * 2 * cols
    row = np.arange(rows).reshape(peers, 2, cols)
    by_peer = np.eye(rows)[row.transpose(1, 0, 2).reshape(-1)]
    by_col = np.eye(rows)[row.transpose(1, 2, 0).reshape(-1)]
    return [jnp.asarray(m, BF16) for m in (by_peer.T, by_col, by_col.T, by_peer)]


def greet(axis_sizes):
    barrier = pltpu.get_barrier_semaphore()
    for axis, n in axis_sizes:
        me = lax.axis_index(axis)

        def tell(k, carry, axis=axis, n=n, me=me):
            pl.semaphore_signal(
                barrier, inc=1, device_id={axis: (me + k) % n}, device_id_type=pl.DeviceIdType.MESH
            )
            return carry

        lax.fori_loop(1, n, tell, 0)


def greeted(axis_sizes):
    pl.semaphore_wait(pltpu.get_barrier_semaphore(), sum(n - 1 for _, n in axis_sizes))


def remote(src, dst, send, recv, axis, peer):
    return pltpu.make_async_remote_copy(
        src_ref=src,
        dst_ref=dst,
        send_sem=send,
        recv_sem=recv,
        device_id={axis: peer},
        device_id_type=pl.DeviceIdType.MESH,
    )


def start_exchange(src, dst, sems, n, spans):
    me = lax.axis_index("tensor")

    def push(i, carry):
        step = (i % 8 // 2) * (n // 4) + ((i // 8 + n // 16) % (n // 8)) * 2 + i % 2
        peer = (me + step) % n
        remote(src.at[peer], dst.at[me], sems.at[0], sems.at[1], "tensor", peer).start()
        return carry

    for lo, hi in spans:
        lax.fori_loop(lo, hi, push, 0)


def keep_own(src, dst, sems):
    me = lax.axis_index("tensor")
    return pltpu.make_async_copy(src.at[me], dst.at[me], sems.at[2])


def end_exchange(src, dst, sems, n):
    keep_own(src, dst, sems).wait()
    span = pl.ds(0, n - 1)
    all_of = remote(src.at[span], dst.at[span], sems.at[0], sems.at[1], "tensor", 0)
    all_of.wait_recv()
    all_of.wait_send()


def sum_scatter(flat, land, sems, ny):
    me = lax.axis_index("dp")
    y, half = me // 2, me % 2

    def push(k, carry):
        peer = (y + k) % ny
        remote(flat.at[peer], land.at[y], sems.at[0], sems.at[1], "dp", peer * 2 + half).start()
        return carry

    lax.fori_loop(1, ny, push, 0)
    land[pl.ds(y, 1)] = flat[pl.ds(y, 1)]


def sum_swap(flat, land, pair, sems, ny):
    me = lax.axis_index("dp")
    span = pl.ds(0, ny - 1)
    first = remote(flat.at[span], land.at[span], sems.at[0], sems.at[1], "dp", 0)
    first.wait_recv()
    acc = land[0].astype(F32)
    for k in range(1, ny):
        acc = acc + land[k].astype(F32)
    pair[0] = acc.astype(BF16)
    other = me // 2 * 2 + (1 - me % 2)
    remote(pair.at[0], pair.at[1], sems.at[2], sems.at[3], "dp", other).start()
    first.wait_send()


def sum_spread(pair, total, gath, sems, ny):
    me = lax.axis_index("dp")
    y, half = me // 2, me % 2
    swap = remote(pair.at[0], pair.at[1], sems.at[2], sems.at[3], "dp", 0)
    swap.wait_recv()
    acc = (pair[0].astype(F32) + pair[1].astype(F32)).astype(BF16)
    total[...] = acc
    gath[pl.ds(y, 1)] = acc[None]

    def push(k, carry):
        peer = (y + k) % ny
        remote(total, gath.at[y], sems.at[4], sems.at[5], "dp", peer * 2 + half).start()
        return carry

    lax.fori_loop(1, ny, push, 0)
    swap.wait_send()


def sum_end(gath, out, sems, ny):
    span = pl.ds(0, ny - 1)
    last = remote(gath.at[span], gath.at[span], sems.at[4], sems.at[5], "dp", 0)
    last.wait_recv()
    for m in range(out.shape[0]):
        out[m] = gath[:, m].astype(F32).reshape(out.shape[1:])
    last.wait_send()


def dot_nt(a, b):
    return lax.dot_general(a, b, (((1,), (1,)), ((), ())), preferred_element_type=F32)


def dot(a, b):
    return jnp.dot(a, b, preferred_element_type=F32)


def dot_tn(a, b):
    return lax.dot_general(a, b, (((0,), (0,)), ((), ())), preferred_element_type=F32)


def whole_kernel(
    n, g, tok, og, fu, su, fdt, sd, pack_in, unpack_mid, pack_mid, unpack_end,
    zdu, mids, ends,
    src, dst, src2, dst2, cols_x, act, dpre,
    flat, land, pair, total, gath, flat2, land2, pair2, total2, gath2,
    links, links2, sums, sums2,
):
    axes = (("tensor", n), ("dp", g))
    ny = g // 2
    cols, _, hidden = su.shape
    t, width = tok.shape
    rows = flat.shape[2]
    step = 256
    greet(axes)
    for c in range(0, t, step):
        span = pl.ds(c, step)
        u = lax.dot_general(fu[0], tok[span], (((0,), (1,)), ((), ())), preferred_element_type=F32)
        dz = dot_nt(sd[0], og[span])
        both = jnp.concatenate([u, dz], axis=0).astype(BF16)
        src[:, :, span] = dot(pack_in[...], both).astype(BF16).reshape(n, 2 * cols, step)
    greeted(axes)
    start_exchange(src, dst, links, n, ((0, n // 2), (n // 2 + 1, n)))
    keep_own(src, dst, links).start()
    end_exchange(src, dst, links, n)

    for c in range(0, t, step):
        span = pl.ds(c, step)
        x = dst[:, :, span].reshape(n * 2 * cols, step)
        x = dot(unpack_mid[...], x).astype(BF16)
        cols_x[:, span] = x
        zs, dus = [], []
        for j in range(cols):
            u = x[j * n : (j + 1) * n]
            dz = x[(cols + j) * n : (cols + j + 1) * n]
            pre = dot_tn(su[j], u).astype(BF16).astype(F32)
            phi = cdf_part(pre)
            a = (pre * phi).astype(BF16)
            slope = phi + pre * jnp.exp(-0.5 * pre * pre) / math.sqrt(2.0 * math.pi)
            d = (dot_tn(fdt[j], dz) * slope).astype(BF16)
            act[j, :, span] = a
            dpre[j, :, span] = d
            zs.append(dot(fdt[j], a))
            dus.append(dot(su[j], d))
        back = jnp.concatenate(zs + dus, axis=0).astype(BF16)
        src2[:, :, span] = dot(pack_mid[...], back).astype(BF16).reshape(n, 2 * cols, step)
    start_exchange(src2, dst2, links2, n, ((0, n // 4), (n // 2 + 1, n)))
    keep_own(src2, dst2, links2).start()

    for j in range(cols):
        u = cols_x[j * n : (j + 1) * n]
        dz = cols_x[(cols + j) * n : (cols + j + 1) * n]
        flat[:, j] = dot_nt(u, dpre[j]).reshape(ny, rows, hidden).astype(BF16)
        flat[:, cols + j] = dot_nt(dz, act[j]).reshape(ny, rows, hidden).astype(BF16)
    sum_scatter(flat, land, sums, ny)
    sum_swap(flat, land, pair, sums, ny)
    start_exchange(src2, dst2, links2, n, ((n // 4, n // 2),))
    sum_spread(pair, total, gath, sums, ny)
    sum_end(gath, mids, sums, ny)
    end_exchange(src2, dst2, links2, n)

    r = dot(unpack_end[...], dst2[...].reshape(n * 2 * cols, t)).astype(BF16)
    flat2[:, 0] = dot(r[:width], og[...]).reshape(ny, width // ny, width).astype(BF16)
    flat2[:, 1] = dot(r[width:], tok[...]).T.reshape(ny, width // ny, width).astype(BF16)
    sum_scatter(flat2, land2, sums2, ny)
    zdu[...] = r
    sum_swap(flat2, land2, pair2, sums2, ny)
    sum_spread(pair2, total2, gath2, sums2, ny)
    sum_end(gath2, ends, sums2, ny)


def sum_scratch(ny, mats, rows, width):
    return [
        pltpu.VMEM((ny, mats, rows, width), BF16),
        pltpu.VMEM((ny, mats, rows, width), BF16),
        pltpu.VMEM((2, mats, rows, width), BF16),
        pltpu.VMEM((mats, rows, width), BF16),
        pltpu.VMEM((ny, mats, rows, width), BF16),
    ]


def kernel_call(body, ins, outs, scratch, ident):
    vmem = pl.BlockSpec(memory_space=pltpu.VMEM)
    return pl.pallas_call(
        body,
        out_shape=outs,
        in_specs=[vmem] * len(ins),
        out_specs=[vmem] * len(outs),
        scratch_shapes=scratch,
        compiler_params=pltpu.CompilerParams(collective_id=ident, has_side_effects=True),
    )(*ins)


def shards(tokens, first_up, second_up, first_down, second_down, out_grad):
    peers = lax.axis_size("tensor")
    groups = lax.axis_size("dp")
    t, width = tokens.shape
    cols, _, hidden = second_up.shape
    ny = groups // 2
    rows = peers * 2 * cols
    block = pltpu.VMEM((peers, 2 * cols, t), BF16)
    links = pltpu.SemaphoreType.DMA((3,))
    sums = pltpu.SemaphoreType.DMA((6,))
    zdu, mids, ends = kernel_call(
        functools.partial(whole_kernel, peers, groups),
        [tokens, out_grad, first_up, second_up, first_down.swapaxes(1, 2), second_down]
        + row_orders(peers, cols),
        [
            jax.ShapeDtypeStruct((rows, t), BF16),
            jax.ShapeDtypeStruct((2 * cols, peers, hidden), F32),
            jax.ShapeDtypeStruct((2, width, width), F32),
        ],
        [
            block,
            block,
            block,
            block,
            pltpu.VMEM((rows, t), BF16),
            pltpu.VMEM((cols, hidden, t), BF16),
            pltpu.VMEM((cols, hidden, t), BF16),
        ]
        + sum_scratch(ny, 2 * cols, peers // ny, hidden)
        + sum_scratch(ny, 2, width // ny, width)
        + [links, links, sums, sums],
        0,
    )
    output = jnp.einsum("jt,jk->tk", zdu[:width], second_down[0], preferred_element_type=F32)
    tok_grad = jnp.einsum("jt,ij->ti", zdu[width:], first_up[0], preferred_element_type=F32)
    return (
        output.astype(BF16),
        tok_grad.astype(BF16),
        ends[1:],
        mids[:cols],
        mids[cols:].swapaxes(1, 2),
        ends[:1],
    )


def solution(mesh):
    cols = P("dp", "tensor")
    blocks = P("tensor", None, None)
    return jax.shard_map(
        shards,
        mesh=mesh,
        in_specs=(cols, blocks, blocks, blocks, blocks, cols),
        out_specs=(cols, cols, blocks, blocks, blocks, blocks),
        check_vma=False,
    )
```

```python
import functools
import math

import jax
import jax.numpy as jnp
import numpy as np
from jax import lax
from jax.experimental import pallas as pl
from jax.experimental.pallas import tpu as pltpu
from jax.sharding import PartitionSpec as P

F32 = jnp.float32
BF16 = jnp.bfloat16


def cdf_part(value):
    return 0.5 * (1.0 + jax.scipy.special.erf(value / math.sqrt(2.0)))


def row_orders(peers, cols):
    rows = peers * 2 * cols
    row = np.arange(rows).reshape(peers, 2, cols)
    by_peer = np.eye(rows)[row.transpose(1, 0, 2).reshape(-1)]
    by_col = np.eye(rows)[row.transpose(1, 2, 0).reshape(-1)]
    return [jnp.asarray(m, BF16) for m in (by_peer.T, by_col, by_col.T, by_peer)]


def greet(axis_sizes):
    barrier = pltpu.get_barrier_semaphore()
    for axis, n in axis_sizes:
        me = lax.axis_index(axis)

        def tell(k, carry, axis=axis, n=n, me=me):
            pl.semaphore_signal(
                barrier, inc=1, device_id={axis: (me + k) % n}, device_id_type=pl.DeviceIdType.MESH
            )
            return carry

        lax.fori_loop(1, n, tell, 0)


def greeted(axis_sizes):
    pl.semaphore_wait(pltpu.get_barrier_semaphore(), sum(n - 1 for _, n in axis_sizes))


def remote(src, dst, send, recv, axis, peer):
    return pltpu.make_async_remote_copy(
        src_ref=src,
        dst_ref=dst,
        send_sem=send,
        recv_sem=recv,
        device_id={axis: peer},
        device_id_type=pl.DeviceIdType.MESH,
    )


def start_exchange(src, dst, sems, n, spans):
    me = lax.axis_index("tensor")

    def push(i, carry):
        step = (i % 8 // 2) * (n // 4) + ((i // 8 + n // 16) % (n // 8)) * 2 + i % 2
        peer = (me + step) % n
        remote(src.at[peer], dst.at[me], sems.at[0], sems.at[1], "tensor", peer).start()
        return carry

    for lo, hi in spans:
        lax.fori_loop(lo, hi, push, 0)


def keep_own(src, dst, sems):
    me = lax.axis_index("tensor")
    return pltpu.make_async_copy(src.at[me], dst.at[me], sems.at[2])


def end_exchange(src, dst, sems, n):
    keep_own(src, dst, sems).wait()
    span = pl.ds(0, n - 1)
    all_of = remote(src.at[span], dst.at[span], sems.at[0], sems.at[1], "tensor", 0)
    all_of.wait_recv()
    all_of.wait_send()


def sum_scatter(flat, land, sems, ny):
    me = lax.axis_index("dp")
    y, half = me // 2, me % 2

    def push(k, carry):
        peer = (y + k) % ny
        remote(flat.at[peer], land.at[y], sems.at[0], sems.at[1], "dp", peer * 2 + half).start()
        return carry

    lax.fori_loop(1, ny, push, 0)
    land[pl.ds(y, 1)] = flat[pl.ds(y, 1)]


def sum_swap(flat, land, pair, sems, ny):
    me = lax.axis_index("dp")
    span = pl.ds(0, ny - 1)
    first = remote(flat.at[span], land.at[span], sems.at[0], sems.at[1], "dp", 0)
    first.wait_recv()
    acc = land[0].astype(F32)
    for k in range(1, ny):
        acc = acc + land[k].astype(F32)
    pair[0] = acc.astype(BF16)
    other = me // 2 * 2 + (1 - me % 2)
    remote(pair.at[0], pair.at[1], sems.at[2], sems.at[3], "dp", other).start()
    first.wait_send()


def sum_spread(pair, total, gath, sems, ny):
    me = lax.axis_index("dp")
    y, half = me // 2, me % 2
    swap = remote(pair.at[0], pair.at[1], sems.at[2], sems.at[3], "dp", 0)
    swap.wait_recv()
    acc = (pair[0].astype(F32) + pair[1].astype(F32)).astype(BF16)
    total[...] = acc
    gath[pl.ds(y, 1)] = acc[None]

    def push(k, carry):
        peer = (y + k) % ny
        remote(total, gath.at[y], sems.at[4], sems.at[5], "dp", peer * 2 + half).start()
        return carry

    lax.fori_loop(1, ny, push, 0)
    swap.wait_send()


def sum_end(gath, out, sems, ny):
    span = pl.ds(0, ny - 1)
    last = remote(gath.at[span], gath.at[span], sems.at[4], sems.at[5], "dp", 0)
    last.wait_recv()
    for m in range(out.shape[0]):
        out[m] = gath[:, m].astype(F32).reshape(out.shape[1:])
    last.wait_send()


def dot_nt(a, b):
    return lax.dot_general(a, b, (((1,), (1,)), ((), ())), preferred_element_type=F32)


def dot(a, b):
    return jnp.dot(a, b, preferred_element_type=F32)


def dot_tn(a, b):
    return lax.dot_general(a, b, (((0,), (0,)), ((), ())), preferred_element_type=F32)


def whole_kernel(
    n, g, tok, og, fu, su, fdt, sd, pack_in, unpack_mid, pack_mid, unpack_end,
    zdu, mids, ends,
    src, dst, src2, dst2, cols_x, act, dpre,
    flat, land, pair, total, gath, flat2, land2, pair2, total2, gath2,
    sums, sums2, *links,
):
    axes = (("tensor", n), ("dp", g))
    ny = g // 2
    cols, _, hidden = su.shape
    t, width = tok.shape
    rows = flat.shape[2]
    parts = src.shape[0]
    part = t // parts
    step = 256
    there, back_again = links[:parts], links[parts:]

    def middle(h, c):
        inner = pl.ds(c, step)
        span = pl.ds(h * part + c, step)
        x = dst[h, :, :, inner].reshape(n * 2 * cols, step)
        x = dot(unpack_mid[...], x).astype(BF16)
        cols_x[:, span] = x
        zs, dus = [], []
        for j in range(cols):
            u = x[j * n : (j + 1) * n]
            dz = x[(cols + j) * n : (cols + j + 1) * n]
            pre = dot_tn(su[j], u).astype(BF16).astype(F32)
            phi = cdf_part(pre)
            a = (pre * phi).astype(BF16)
            slope = phi + pre * jnp.exp(-0.5 * pre * pre) / math.sqrt(2.0 * math.pi)
            d = (dot_tn(fdt[j], dz) * slope).astype(BF16)
            act[j, :, span] = a
            dpre[j, :, span] = d
            zs.append(dot(fdt[j], a))
            dus.append(dot(su[j], d))
        back = jnp.concatenate(zs + dus, axis=0).astype(BF16)
        src2[h, :, :, inner] = dot(pack_mid[...], back).astype(BF16).reshape(n, 2 * cols, step)

    greet(axes)
    for c in range(0, t, step):
        span = pl.ds(c, step)
        u = lax.dot_general(fu[0], tok[span], (((0,), (1,)), ((), ())), preferred_element_type=F32)
        dz = dot_nt(sd[0], og[span])
        both = jnp.concatenate([u, dz], axis=0).astype(BF16)
        both = dot(pack_in[...], both).astype(BF16).reshape(n, 2 * cols, step)
        src[c // part, :, :, pl.ds(c % part, step)] = both
    greeted(axes)
    for h in range(parts):
        start_exchange(src.at[h], dst.at[h], there[h], n, ((0, n // 2), (n // 2 + 1, n)))
        keep_own(src.at[h], dst.at[h], there[h]).start()
    for h in range(parts):
        end_exchange(src.at[h], dst.at[h], there[h], n)
        for c in range(0, part, step):
            middle(h, c)
        last = h == parts - 1
        spans = ((0, n // 4 if last else n // 2), (n // 2 + 1, n))
        start_exchange(src2.at[h], dst2.at[h], back_again[h], n, spans)
        keep_own(src2.at[h], dst2.at[h], back_again[h]).start()

    for j in range(cols):
        u = cols_x[j * n : (j + 1) * n]
        dz = cols_x[(cols + j) * n : (cols + j + 1) * n]
        flat[:, j] = dot_nt(u, dpre[j]).reshape(ny, rows, hidden).astype(BF16)
        flat[:, cols + j] = dot_nt(dz, act[j]).reshape(ny, rows, hidden).astype(BF16)
    sum_scatter(flat, land, sums, ny)
    sum_swap(flat, land, pair, sums, ny)
    h = parts - 1
    start_exchange(src2.at[h], dst2.at[h], back_again[h], n, ((n // 4, n // 2),))

    down = jnp.zeros((width, width), F32)
    up = jnp.zeros((width, width), F32)
    for h in range(parts):
        if h == parts - 1:
            sum_spread(pair, total, gath, sums, ny)
            sum_end(gath, mids, sums, ny)
        end_exchange(src2.at[h], dst2.at[h], back_again[h], n)
        span = pl.ds(h * part, part)
        r = dot(unpack_end[...], dst2[h].reshape(n * 2 * cols, part)).astype(BF16)
        zdu[:, span] = r
        down = down + dot(r[:width], og[span])
        up = up + dot(r[width:], tok[span])
    flat2[:, 0] = down.reshape(ny, width // ny, width).astype(BF16)
    flat2[:, 1] = up.T.reshape(ny, width // ny, width).astype(BF16)
    sum_scatter(flat2, land2, sums2, ny)
    sum_swap(flat2, land2, pair2, sums2, ny)
    sum_spread(pair2, total2, gath2, sums2, ny)
    sum_end(gath2, ends, sums2, ny)


def sum_scratch(ny, mats, rows, width):
    return [
        pltpu.VMEM((ny, mats, rows, width), BF16),
        pltpu.VMEM((ny, mats, rows, width), BF16),
        pltpu.VMEM((2, mats, rows, width), BF16),
        pltpu.VMEM((mats, rows, width), BF16),
        pltpu.VMEM((ny, mats, rows, width), BF16),
    ]


def kernel_call(body, ins, outs, scratch, ident):
    vmem = pl.BlockSpec(memory_space=pltpu.VMEM)
    return pl.pallas_call(
        body,
        out_shape=outs,
        in_specs=[vmem] * len(ins),
        out_specs=[vmem] * len(outs),
        scratch_shapes=scratch,
        compiler_params=pltpu.CompilerParams(collective_id=ident, has_side_effects=True),
    )(*ins)


def shards(tokens, first_up, second_up, first_down, second_down, out_grad):
    peers = lax.axis_size("tensor")
    groups = lax.axis_size("dp")
    t, width = tokens.shape
    cols, _, hidden = second_up.shape
    ny = groups // 2
    rows = peers * 2 * cols
    parts = 2
    block = pltpu.VMEM((parts, peers, 2 * cols, t // parts), BF16)
    links = pltpu.SemaphoreType.DMA((3,))
    sums = pltpu.SemaphoreType.DMA((6,))
    zdu, mids, ends = kernel_call(
        functools.partial(whole_kernel, peers, groups),
        [tokens, out_grad, first_up, second_up, first_down.swapaxes(1, 2), second_down]
        + row_orders(peers, cols),
        [
            jax.ShapeDtypeStruct((rows, t), BF16),
            jax.ShapeDtypeStruct((2 * cols, peers, hidden), F32),
            jax.ShapeDtypeStruct((2, width, width), F32),
        ],
        [
            block,
            block,
            block,
            block,
            pltpu.VMEM((rows, t), BF16),
            pltpu.VMEM((cols, hidden, t), BF16),
            pltpu.VMEM((cols, hidden, t), BF16),
        ]
        + sum_scratch(ny, 2 * cols, peers // ny, hidden)
        + sum_scratch(ny, 2, width // ny, width)
        + [sums, sums]
        + [links] * (2 * parts),
        0,
    )
    output = jnp.einsum("jt,jk->tk", zdu[:width], second_down[0], preferred_element_type=F32)
    tok_grad = jnp.einsum("jt,ij->ti", zdu[width:], first_up[0], preferred_element_type=F32)
    return (
        output.astype(BF16),
        tok_grad.astype(BF16),
        ends[1:],
        mids[:cols],
        mids[cols:].swapaxes(1, 2),
        ends[:1],
    )


def solution(mesh):
    cols = P("dp", "tensor")
    blocks = P("tensor", None, None)
    return jax.shard_map(
        shards,
        mesh=mesh,
        in_specs=(cols, blocks, blocks, blocks, blocks, cols),
        out_specs=(cols, cols, blocks, blocks, blocks, blocks),
        check_vma=False,
    )
```

```python
import functools
import math

import jax
import jax.numpy as jnp
import numpy as np
from jax import lax
from jax.experimental import pallas as pl
from jax.experimental.pallas import tpu as pltpu
from jax.sharding import PartitionSpec as P

F32 = jnp.float32
BF16 = jnp.bfloat16


def cdf_part(value):
    return 0.5 * (1.0 + jax.scipy.special.erf(value / math.sqrt(2.0)))


def row_orders(peers, cols):
    rows = peers * 2 * cols
    row = np.arange(rows).reshape(peers, 2, cols)
    by_peer = np.eye(rows)[row.transpose(1, 0, 2).reshape(-1)]
    by_col = np.eye(rows)[row.transpose(1, 2, 0).reshape(-1)]
    return [jnp.asarray(m, BF16) for m in (by_peer.T, by_col, by_col.T, by_peer)]


def greet(axis_sizes):
    barrier = pltpu.get_barrier_semaphore()
    for axis, n in axis_sizes:
        me = lax.axis_index(axis)

        def tell(k, carry, axis=axis, n=n, me=me):
            pl.semaphore_signal(
                barrier, inc=1, device_id={axis: (me + n // 2 + k) % n}, device_id_type=pl.DeviceIdType.MESH
            )
            return carry

        lax.fori_loop(0, n // 2, tell, 0)
        lax.fori_loop(n // 2 + 1, n, tell, 0)


def greeted(axis_sizes):
    pl.semaphore_wait(pltpu.get_barrier_semaphore(), sum(n - 1 for _, n in axis_sizes))


def remote(src, dst, send, recv, axis, peer):
    return pltpu.make_async_remote_copy(
        src_ref=src,
        dst_ref=dst,
        send_sem=send,
        recv_sem=recv,
        device_id={axis: peer},
        device_id_type=pl.DeviceIdType.MESH,
    )


def start_exchange(src, dst, sems, n, spans):
    me = lax.axis_index("tensor")

    def push(i, carry):
        step = (i % 8 // 2) * (n // 4) + ((i // 8 + n // 16) % (n // 8)) * 2 + i % 2
        peer = (me + step) % n
        remote(src.at[peer], dst.at[me], sems.at[0], sems.at[1], "tensor", peer).start()
        return carry

    for lo, hi in spans:
        lax.fori_loop(lo, hi, push, 0)


def keep_own(src, dst, sems):
    me = lax.axis_index("tensor")
    return pltpu.make_async_copy(src.at[me], dst.at[me], sems.at[2])


def end_exchange(src, dst, sems, n):
    keep_own(src, dst, sems).wait()
    span = pl.ds(0, n - 1)
    all_of = remote(src.at[span], dst.at[span], sems.at[0], sems.at[1], "tensor", 0)
    all_of.wait_recv()
    all_of.wait_send()


def sum_scatter(flat, land, sems, ny):
    me = lax.axis_index("dp")
    y, half = me // 2, me % 2

    def push(k, carry):
        peer = (y + k) % ny
        remote(flat.at[peer], land.at[y], sems.at[0], sems.at[1], "dp", peer * 2 + half).start()
        return carry

    lax.fori_loop(1, ny, push, 0)
    land[pl.ds(y, 1)] = flat[pl.ds(y, 1)]


def sum_swap(flat, land, pair, sems, ny):
    me = lax.axis_index("dp")
    span = pl.ds(0, ny - 1)
    first = remote(flat.at[span], land.at[span], sems.at[0], sems.at[1], "dp", 0)
    first.wait_recv()
    acc = land[0].astype(F32)
    for k in range(1, ny):
        acc = acc + land[k].astype(F32)
    pair[0] = acc.astype(BF16)
    other = me // 2 * 2 + (1 - me % 2)
    remote(pair.at[0], pair.at[1], sems.at[2], sems.at[3], "dp", other).start()
    first.wait_send()


def sum_spread(pair, total, gath, sems, ny):
    me = lax.axis_index("dp")
    y, half = me // 2, me % 2
    swap = remote(pair.at[0], pair.at[1], sems.at[2], sems.at[3], "dp", 0)
    swap.wait_recv()
    acc = (pair[0].astype(F32) + pair[1].astype(F32)).astype(BF16)
    total[...] = acc
    gath[pl.ds(y, 1)] = acc[None]

    def push(k, carry):
        peer = (y + k) % ny
        remote(total, gath.at[y], sems.at[4], sems.at[5], "dp", peer * 2 + half).start()
        return carry

    lax.fori_loop(1, ny, push, 0)
    swap.wait_send()


def sum_end(gath, out, sems, ny):
    span = pl.ds(0, ny - 1)
    last = remote(gath.at[span], gath.at[span], sems.at[4], sems.at[5], "dp", 0)
    last.wait_recv()
    for m in range(out.shape[0]):
        out[m] = gath[:, m].astype(F32).reshape(out.shape[1:])
    last.wait_send()


def dot_nt(a, b):
    return lax.dot_general(a, b, (((1,), (1,)), ((), ())), preferred_element_type=F32)


def dot(a, b):
    return jnp.dot(a, b, preferred_element_type=F32)


def dot_tn(a, b):
    return lax.dot_general(a, b, (((0,), (0,)), ((), ())), preferred_element_type=F32)


def whole_kernel(
    n, g, tok, og, fu, su, fdt, sd, pack_in, unpack_mid, pack_mid, unpack_end,
    zdu, mids, ends,
    src, dst, src2, dst2, cols_x, act, dpre,
    flat, land, pair, total, gath, flat2, land2, pair2, total2, gath2,
    sums, sums2, *links,
):
    axes = (("dp", g), ("tensor", n))
    ny = g // 2
    cols, _, hidden = su.shape
    t, width = tok.shape
    rows = flat.shape[2]
    parts = src.shape[0]
    part = t // parts
    step = 256
    there, back_again = links[:parts], links[parts:]

    def middle(h, c):
        inner = pl.ds(c, step)
        span = pl.ds(h * part + c, step)
        x = dst[h, :, :, inner].reshape(n * 2 * cols, step)
        x = dot(unpack_mid[...], x).astype(BF16)
        cols_x[:, span] = x
        zs, dus = [], []
        for j in range(cols):
            u = x[j * n : (j + 1) * n]
            dz = x[(cols + j) * n : (cols + j + 1) * n]
            pre = dot_tn(su[j], u).astype(BF16).astype(F32)
            phi = cdf_part(pre)
            a = (pre * phi).astype(BF16)
            slope = phi + pre * jnp.exp(-0.5 * pre * pre) / math.sqrt(2.0 * math.pi)
            d = (dot_tn(fdt[j], dz) * slope).astype(BF16)
            act[j, :, span] = a
            dpre[j, :, span] = d
            zs.append(dot(fdt[j], a))
            dus.append(dot(su[j], d))
        back = jnp.concatenate(zs + dus, axis=0).astype(BF16)
        src2[h, :, :, inner] = dot(pack_mid[...], back).astype(BF16).reshape(n, 2 * cols, step)

    greet(axes)
    for c in range(0, t, step):
        span = pl.ds(c, step)
        u = lax.dot_general(fu[0], tok[span], (((0,), (1,)), ((), ())), preferred_element_type=F32)
        dz = dot_nt(sd[0], og[span])
        both = jnp.concatenate([u, dz], axis=0).astype(BF16)
        both = dot(pack_in[...], both).astype(BF16).reshape(n, 2 * cols, step)
        src[c // part, :, :, pl.ds(c % part, step)] = both
    greeted(axes)
    for h in range(parts):
        start_exchange(src.at[h], dst.at[h], there[h], n, ((0, n // 2), (n // 2 + 1, n)))
        keep_own(src.at[h], dst.at[h], there[h]).start()
    for h in range(parts):
        end_exchange(src.at[h], dst.at[h], there[h], n)
        for c in range(0, part, step):
            middle(h, c)
        last = h == parts - 1
        spans = ((0, n // 4 if last else n // 2), (n // 2 + 1, n))
        start_exchange(src2.at[h], dst2.at[h], back_again[h], n, spans)
        keep_own(src2.at[h], dst2.at[h], back_again[h]).start()

    for j in range(cols):
        u = cols_x[j * n : (j + 1) * n]
        dz = cols_x[(cols + j) * n : (cols + j + 1) * n]
        flat[:, j] = dot_nt(u, dpre[j]).reshape(ny, rows, hidden).astype(BF16)
        flat[:, cols + j] = dot_nt(dz, act[j]).reshape(ny, rows, hidden).astype(BF16)
    sum_scatter(flat, land, sums, ny)
    sum_swap(flat, land, pair, sums, ny)
    h = parts - 1
    start_exchange(src2.at[h], dst2.at[h], back_again[h], n, ((n // 4, n // 2),))

    down = jnp.zeros((width, width), F32)
    up = jnp.zeros((width, width), F32)
    for h in range(parts):
        if h == parts - 1:
            sum_spread(pair, total, gath, sums, ny)
            sum_end(gath, mids, sums, ny)
        end_exchange(src2.at[h], dst2.at[h], back_again[h], n)
        span = pl.ds(h * part, part)
        r = dot(unpack_end[...], dst2[h].reshape(n * 2 * cols, part)).astype(BF16)
        zdu[:, span] = r
        down = down + dot(r[:width], og[span])
        up = up + dot(r[width:], tok[span])
    flat2[:, 0] = down.reshape(ny, width // ny, width).astype(BF16)
    flat2[:, 1] = up.T.reshape(ny, width // ny, width).astype(BF16)
    sum_scatter(flat2, land2, sums2, ny)
    sum_swap(flat2, land2, pair2, sums2, ny)
    sum_spread(pair2, total2, gath2, sums2, ny)
    sum_end(gath2, ends, sums2, ny)


def sum_scratch(ny, mats, rows, width):
    return [
        pltpu.VMEM((ny, mats, rows, width), BF16),
        pltpu.VMEM((ny, mats, rows, width), BF16),
        pltpu.VMEM((2, mats, rows, width), BF16),
        pltpu.VMEM((mats, rows, width), BF16),
        pltpu.VMEM((ny, mats, rows, width), BF16),
    ]


def kernel_call(body, ins, outs, scratch, ident):
    vmem = pl.BlockSpec(memory_space=pltpu.VMEM)
    return pl.pallas_call(
        body,
        out_shape=outs,
        in_specs=[vmem] * len(ins),
        out_specs=[vmem] * len(outs),
        scratch_shapes=scratch,
        compiler_params=pltpu.CompilerParams(collective_id=ident, has_side_effects=True),
    )(*ins)


def shards(tokens, first_up, second_up, first_down, second_down, out_grad):
    peers = lax.axis_size("tensor")
    groups = lax.axis_size("dp")
    t, width = tokens.shape
    cols, _, hidden = second_up.shape
    ny = groups // 2
    rows = peers * 2 * cols
    parts = 4
    block = pltpu.VMEM((parts, peers, 2 * cols, t // parts), BF16)
    links = pltpu.SemaphoreType.DMA((3,))
    sums = pltpu.SemaphoreType.DMA((6,))
    zdu, mids, ends = kernel_call(
        functools.partial(whole_kernel, peers, groups),
        [tokens, out_grad, first_up, second_up, first_down.swapaxes(1, 2), second_down]
        + row_orders(peers, cols),
        [
            jax.ShapeDtypeStruct((rows, t), BF16),
            jax.ShapeDtypeStruct((2 * cols, peers, hidden), F32),
            jax.ShapeDtypeStruct((2, width, width), F32),
        ],
        [
            block,
            block,
            block,
            block,
            pltpu.VMEM((rows, t), BF16),
            pltpu.VMEM((cols, hidden, t), BF16),
            pltpu.VMEM((cols, hidden, t), BF16),
        ]
        + sum_scratch(ny, 2 * cols, peers // ny, hidden)
        + sum_scratch(ny, 2, width // ny, width)
        + [sums, sums]
        + [links] * (2 * parts),
        0,
    )
    output = jnp.einsum("jt,jk->tk", zdu[:width], second_down[0], preferred_element_type=F32)
    tok_grad = jnp.einsum("jt,ij->ti", zdu[width:], first_up[0], preferred_element_type=F32)
    return (
        output.astype(BF16),
        tok_grad.astype(BF16),
        ends[1:],
        mids[:cols],
        mids[cols:].swapaxes(1, 2),
        ends[:1],
    )


def solution(mesh):
    cols = P("dp", "tensor")
    blocks = P("tensor", None, None)
    return jax.shard_map(
        shards,
        mesh=mesh,
        in_specs=(cols, blocks, blocks, blocks, blocks, cols),
        out_specs=(cols, cols, blocks, blocks, blocks, blocks),
        check_vma=False,
    )
```

```python
import functools
import math

import jax
import jax.numpy as jnp
import numpy as np
from jax import lax
from jax.experimental import pallas as pl
from jax.experimental.pallas import tpu as pltpu
from jax.sharding import PartitionSpec as P

F32 = jnp.float32
BF16 = jnp.bfloat16


def cdf_part(value):
    return 0.5 * (1.0 + jax.scipy.special.erf(value / math.sqrt(2.0)))


def row_orders(peers, cols):
    rows = peers * 2 * cols
    row = np.arange(rows).reshape(peers, 2, cols)
    by_peer = np.eye(rows)[row.transpose(1, 0, 2).reshape(-1)]
    by_col = np.eye(rows)[row.transpose(1, 2, 0).reshape(-1)]
    return [jnp.asarray(m, BF16) for m in (by_peer.T, by_col, by_col.T, by_peer)]


def greet(axis_sizes):
    barrier = pltpu.get_barrier_semaphore()
    for axis, n in axis_sizes:
        me = lax.axis_index(axis)

        def tell(k, carry, axis=axis, n=n, me=me):
            pl.semaphore_signal(
                barrier, inc=1, device_id={axis: (me + n // 2 + k) % n}, device_id_type=pl.DeviceIdType.MESH
            )
            return carry

        lax.fori_loop(0, n // 2, tell, 0)
        lax.fori_loop(n // 2 + 1, n, tell, 0)


def greeted(axis_sizes):
    pl.semaphore_wait(pltpu.get_barrier_semaphore(), sum(n - 1 for _, n in axis_sizes))


def remote(src, dst, send, recv, axis, peer):
    return pltpu.make_async_remote_copy(
        src_ref=src,
        dst_ref=dst,
        send_sem=send,
        recv_sem=recv,
        device_id={axis: peer},
        device_id_type=pl.DeviceIdType.MESH,
    )


def start_exchange(src, dst, sems, n, spans):
    me = lax.axis_index("tensor")

    def push(i, carry):
        step = (i % 8 // 2) * (n // 4) + ((i // 8 + n // 16) % (n // 8)) * 2 + i % 2
        peer = (me + step) % n
        remote(src.at[peer], dst.at[me], sems.at[0], sems.at[1], "tensor", peer).start()
        return carry

    for lo, hi in spans:
        lax.fori_loop(lo, hi, push, 0)


def keep_own(src, dst, sems):
    me = lax.axis_index("tensor")
    return pltpu.make_async_copy(src.at[me], dst.at[me], sems.at[2])


def end_exchange(src, dst, sems, n):
    keep_own(src, dst, sems).wait()
    span = pl.ds(0, n - 1)
    all_of = remote(src.at[span], dst.at[span], sems.at[0], sems.at[1], "tensor", 0)
    all_of.wait_recv()
    all_of.wait_send()


def sum_scatter(flat, land, sems, ny):
    me = lax.axis_index("dp")
    y, half = me // 2, me % 2

    def push(k, carry):
        peer = (y + k) % ny
        remote(flat.at[peer], land.at[y], sems.at[0], sems.at[1], "dp", peer * 2 + half).start()
        return carry

    lax.fori_loop(1, ny, push, 0)
    land[pl.ds(y, 1)] = flat[pl.ds(y, 1)]


def sum_swap(flat, land, pair, sems, ny):
    me = lax.axis_index("dp")
    span = pl.ds(0, ny - 1)
    first = remote(flat.at[span], land.at[span], sems.at[0], sems.at[1], "dp", 0)
    first.wait_recv()
    acc = land[0].astype(F32)
    for k in range(1, ny):
        acc = acc + land[k].astype(F32)
    pair[0] = acc.astype(BF16)
    other = me // 2 * 2 + (1 - me % 2)
    remote(pair.at[0], pair.at[1], sems.at[2], sems.at[3], "dp", other).start()
    first.wait_send()


def sum_spread(pair, total, gath, sems, ny):
    me = lax.axis_index("dp")
    y, half = me // 2, me % 2
    swap = remote(pair.at[0], pair.at[1], sems.at[2], sems.at[3], "dp", 0)
    swap.wait_recv()
    acc = (pair[0].astype(F32) + pair[1].astype(F32)).astype(BF16)
    total[...] = acc
    gath[pl.ds(y, 1)] = acc[None]

    def push(k, carry):
        peer = (y + k) % ny
        remote(total, gath.at[y], sems.at[4], sems.at[5], "dp", peer * 2 + half).start()
        return carry

    lax.fori_loop(1, ny, push, 0)
    swap.wait_send()


def sum_end(gath, out, sems, ny):
    span = pl.ds(0, ny - 1)
    last = remote(gath.at[span], gath.at[span], sems.at[4], sems.at[5], "dp", 0)
    last.wait_recv()
    for m in range(out.shape[0]):
        out[m] = gath[:, m].astype(F32).reshape(out.shape[1:])
    last.wait_send()


def dot_nt(a, b):
    return lax.dot_general(a, b, (((1,), (1,)), ((), ())), preferred_element_type=F32)


def dot(a, b):
    return jnp.dot(a, b, preferred_element_type=F32)


def dot_tn(a, b):
    return lax.dot_general(a, b, (((0,), (0,)), ((), ())), preferred_element_type=F32)


def whole_kernel(
    n, g, tok, og, fu, su, fdt, sd, pack_in, unpack_mid, pack_mid, unpack_end,
    zdu, mids, ends,
    src, dst, src2, dst2, cols_x, act, dpre,
    flat, land, pair, total, gath, flat2, land2, pair2, total2, gath2,
    sums, sums2, *links,
):
    axes = (("dp", g), ("tensor", n))
    ny = g // 2
    cols, _, hidden = su.shape
    t, width = tok.shape
    rows = flat.shape[2]
    parts = src.shape[0]
    part = t // parts
    step = 256
    there, back_again = links[:parts], links[parts:]

    def middle(h, c):
        inner = pl.ds(c, step)
        span = pl.ds(h * part + c, step)
        x = dst[h, :, :, inner].reshape(n * 2 * cols, step)
        x = dot(unpack_mid[...], x).astype(BF16)
        cols_x[:, span] = x
        zs, dus = [], []
        for j in range(cols):
            u = x[j * n : (j + 1) * n]
            dz = x[(cols + j) * n : (cols + j + 1) * n]
            pre = dot_tn(su[j], u).astype(BF16).astype(F32)
            phi = cdf_part(pre)
            a = (pre * phi).astype(BF16)
            slope = phi + pre * jnp.exp(-0.5 * pre * pre) / math.sqrt(2.0 * math.pi)
            d = (dot_tn(fdt[j], dz) * slope).astype(BF16)
            act[j, :, span] = a
            dpre[j, :, span] = d
            zs.append(dot(fdt[j], a))
            dus.append(dot(su[j], d))
        back = jnp.concatenate(zs + dus, axis=0).astype(BF16)
        src2[h, :, :, inner] = dot(pack_mid[...], back).astype(BF16).reshape(n, 2 * cols, step)

    greet(axes)
    for c in range(0, t, step):
        span = pl.ds(c, step)
        u = lax.dot_general(fu[0], tok[span], (((0,), (1,)), ((), ())), preferred_element_type=F32)
        dz = dot_nt(sd[0], og[span])
        both = jnp.concatenate([u, dz], axis=0).astype(BF16)
        both = dot(pack_in[...], both).astype(BF16).reshape(n, 2 * cols, step)
        src[c // part, :, :, pl.ds(c % part, step)] = both
    greeted(axes)
    for h in range(parts):
        start_exchange(src.at[h], dst.at[h], there[h], n, ((0, n // 2), (n // 2 + 1, n)))
        keep_own(src.at[h], dst.at[h], there[h]).start()
    for h in range(parts):
        end_exchange(src.at[h], dst.at[h], there[h], n)
        for c in range(0, part, step):
            middle(h, c)
        last = h == parts - 1
        spans = ((0, 3 * n // 8 if last else n // 2), (n // 2 + 1, n))
        start_exchange(src2.at[h], dst2.at[h], back_again[h], n, spans)
        keep_own(src2.at[h], dst2.at[h], back_again[h]).start()

    for j in range(cols):
        u = cols_x[j * n : (j + 1) * n]
        dz = cols_x[(cols + j) * n : (cols + j + 1) * n]
        flat[:, j] = dot_nt(u, dpre[j]).reshape(ny, rows, hidden).astype(BF16)
        flat[:, cols + j] = dot_nt(dz, act[j]).reshape(ny, rows, hidden).astype(BF16)
    sum_scatter(flat, land, sums, ny)
    sum_swap(flat, land, pair, sums, ny)
    h = parts - 1
    start_exchange(src2.at[h], dst2.at[h], back_again[h], n, ((3 * n // 8, n // 2),))

    down = jnp.zeros((width, width), F32)
    up = jnp.zeros((width, width), F32)
    for h in range(parts):
        if h == parts - 1:
            sum_spread(pair, total, gath, sums, ny)
            sum_end(gath, mids, sums, ny)
        end_exchange(src2.at[h], dst2.at[h], back_again[h], n)
        span = pl.ds(h * part, part)
        r = dot(unpack_end[...], dst2[h].reshape(n * 2 * cols, part)).astype(BF16)
        zdu[:, span] = r
        down = down + dot(r[:width], og[span])
        up = up + dot(r[width:], tok[span])
    flat2[:, 0] = down.reshape(ny, width // ny, width).astype(BF16)
    flat2[:, 1] = up.T.reshape(ny, width // ny, width).astype(BF16)
    sum_scatter(flat2, land2, sums2, ny)
    sum_swap(flat2, land2, pair2, sums2, ny)
    sum_spread(pair2, total2, gath2, sums2, ny)
    sum_end(gath2, ends, sums2, ny)


def sum_scratch(ny, mats, rows, width):
    return [
        pltpu.VMEM((ny, mats, rows, width), BF16),
        pltpu.VMEM((ny, mats, rows, width), BF16),
        pltpu.VMEM((2, mats, rows, width), BF16),
        pltpu.VMEM((mats, rows, width), BF16),
        pltpu.VMEM((ny, mats, rows, width), BF16),
    ]


def kernel_call(body, ins, outs, scratch, ident):
    vmem = pl.BlockSpec(memory_space=pltpu.VMEM)
    return pl.pallas_call(
        body,
        out_shape=outs,
        in_specs=[vmem] * len(ins),
        out_specs=[vmem] * len(outs),
        scratch_shapes=scratch,
        compiler_params=pltpu.CompilerParams(collective_id=ident, has_side_effects=True),
    )(*ins)


def shards(tokens, first_up, second_up, first_down, second_down, out_grad):
    peers = lax.axis_size("tensor")
    groups = lax.axis_size("dp")
    t, width = tokens.shape
    cols, _, hidden = second_up.shape
    ny = groups // 2
    rows = peers * 2 * cols
    parts = 2
    block = pltpu.VMEM((parts, peers, 2 * cols, t // parts), BF16)
    links = pltpu.SemaphoreType.DMA((3,))
    sums = pltpu.SemaphoreType.DMA((6,))
    zdu, mids, ends = kernel_call(
        functools.partial(whole_kernel, peers, groups),
        [tokens, out_grad, first_up, second_up, first_down.swapaxes(1, 2), second_down]
        + row_orders(peers, cols),
        [
            jax.ShapeDtypeStruct((rows, t), BF16),
            jax.ShapeDtypeStruct((2 * cols, peers, hidden), F32),
            jax.ShapeDtypeStruct((2, width, width), F32),
        ],
        [
            block,
            block,
            block,
            block,
            pltpu.VMEM((rows, t), BF16),
            pltpu.VMEM((cols, hidden, t), BF16),
            pltpu.VMEM((cols, hidden, t), BF16),
        ]
        + sum_scratch(ny, 2 * cols, peers // ny, hidden)
        + sum_scratch(ny, 2, width // ny, width)
        + [sums, sums]
        + [links] * (2 * parts),
        0,
    )
    output = jnp.einsum("jt,jk->tk", zdu[:width], second_down[0], preferred_element_type=F32)
    tok_grad = jnp.einsum("jt,ij->ti", zdu[width:], first_up[0], preferred_element_type=F32)
    return (
        output.astype(BF16),
        tok_grad.astype(BF16),
        ends[1:],
        mids[:cols],
        mids[cols:].swapaxes(1, 2),
        ends[:1],
    )


def solution(mesh):
    cols = P("dp", "tensor")
    blocks = P("tensor", None, None)
    return jax.shard_map(
        shards,
        mesh=mesh,
        in_specs=(cols, blocks, blocks, blocks, blocks, cols),
        out_specs=(cols, cols, blocks, blocks, blocks, blocks),
        check_vma=False,
    )
```
